32 devices in a mesh: sec: 8 (over y, x, core), head: 4 (over z).
Axes of the slice: x: 2, y: 2, z: 4, core: 2. Of those that a mesh axis runs over, the one named last changes fastest.
Arguments:
- tokens: bfloat16 [8192, 2048], P('sec', 'head'), may hold values from -6 to 6
- fresh_tokens: bfloat16 [1024, 2048], P(None, 'head'), may hold values from -6 to 6
- route_rows: int32 [8, 4, 128], P('sec'), may hold values from 0 to 255, as said below
- block_list: int32 [8, 4, 16], P('sec'), may hold values from 0 to 31, all different within a row
- norm_gain: float32 [8, 2048], P('sec'), may hold values from 0.25 to 1.75
- route_weight: bfloat16 [8, 2048], P('sec'), may hold values from -0.125 to 0.125
- w_query: bfloat16 [8, 2048, 2048], P('sec', None, 'head'), may hold values from -0.125 to 0.125
- w_key: bfloat16 [8, 2048, 2048], P('sec', None, 'head'), may hold values from -0.26367188 to 0.26367188
- w_value: bfloat16 [8, 2048, 2048], P('sec', None, 'head'), may hold values from -0.125 to 0.125
- w_out: bfloat16 [8, 2048, 2048], P('sec', None, 'head'), may hold values from -0.52734375 to 0.52734375
- cache_keys: bfloat16 [8, 4096, 2048], P('sec', None, 'head'), may hold values from -2400 to 2400
- cache_values: bfloat16 [8, 4096, 2048], P('sec', None, 'head'), may hold values from -6 to 6
Outputs:
- next_input: bfloat16 [8192, 2048], P('sec', 'head')
The draws below stay inside these ranges and needn't reach their ends.
Inputs may be any that keep to these rules, and one draw needn't show every extreme that they name: `route_rows`: within one section and group the 128 entries are distinct row numbers of the group. `block_list`: each section's group names 16 distinct blocks.
All inputs are finite; a program needn't handle non-finite values.
Results may differ from the reference program's by a relative error of at most 0.017.
Values may be sent and summed in bfloat16 or wider, within the bound.
No kernel may reach another device: no remote copies, remote signals or barrier semaphores. Data moves between devices by JAX's collectives and lax.ppermute only.
A program may use at most 128 MiB of HBM per device.

```python
import math
import jax
import jax.numpy as jnp
from jax import lax

D = 2048
HEADS = 32
HEAD_DIM = 64
GROUP = 256
GROUPS = 4
CACHE = 4096
BLOCK = 128
TOK_DEV = 1024
ROUTED_GROUP = 128
CACHE_BLOCKS = 32
PICKED = 16
TOKENS = 8192
N_SEC = 8


def draw_route_rows(key, part):
    row_keys = jax.random.split(jax.random.fold_in(key, 11), N_SEC * GROUPS)
    chosen = jax.vmap(lambda one_key: jax.random.permutation(one_key, GROUP)[:ROUTED_GROUP])(row_keys)
    return chosen.reshape(N_SEC, GROUPS, ROUTED_GROUP).astype(jnp.int32)


def draw_cache_keys(key, part):
    first = jax.random.fold_in(jax.random.fold_in(key, 23), 0)
    shape = (N_SEC, CACHE, HEADS, HEAD_DIM)
    base = jnp.clip(jax.random.normal(first, shape, jnp.float32), -8.0, 8.0) * 2.0
    return base.reshape(N_SEC, CACHE, HEADS * HEAD_DIM).astype(jnp.bfloat16)


def block_scale(stream_key, shape, pieces, smallest, high):
    loudness = 1.0
    for position, parts in pieces:
        steps = jax.random.uniform(jax.random.fold_in(jax.random.fold_in(stream_key, 6), position), (parts,), jnp.float32, smallest / len(pieces), high / len(pieces))
        loudness = loudness * jnp.repeat(jnp.exp(steps), shape[position] // parts).reshape((-1,) + (1,) * (len(shape) - 1 - position))
    return loudness


def choose_distinct(key, rows, number_of, top, lift):
    sequence = jax.random.permutation(jax.random.fold_in(key, 1), number_of)
    pull = sequence
    for power in range(3):
        pull = pull * pull // number_of
    pull = pull * lift // number_of
    chance = jax.random.randint(jax.random.fold_in(key, 2), (rows, number_of), 0, 4096) + pull
    fixed_rows = jax.random.permutation(jax.random.fold_in(key, 3), rows)[jnp.arange(number_of) % rows]
    chance = jnp.where(jnp.arange(rows)[:, None] == fixed_rows[None, :], 1 << 14, chance)
    priority = chance * number_of + jnp.arange(number_of)
    return lax.top_k(priority.astype(jnp.int32), top)[1].astype(jnp.int32)


def gaussian(key, shape, deviation, most, pieces=(), kind=jnp.bfloat16):
    array = jax.random.normal(key, shape, jnp.float32) * deviation
    if len(pieces) > 0:
        array = block_scale(key, shape, pieces, -0.22, 0.18) * array
    return jnp.clip(array, min=-most, max=most).astype(kind)


def setup_inputs(seed: int = 0) -> dict:
    splits = jax.random.split(jax.random.key(seed), 13)
    tokens = gaussian(splits[0], (TOKENS, D), 1.0, 6.0, ((0, 8), (1, 4)))
    fresh_tokens = gaussian(splits[1], (TOK_DEV, D), 1.0, 6.0, ((1, 4),))
    route_rows = draw_route_rows(jax.random.fold_in(splits[12], 71), 0)
    block_list = choose_distinct(splits[3], N_SEC * GROUPS, CACHE_BLOCKS, PICKED, 0).reshape((N_SEC, GROUPS, PICKED))
    norm_gain = jnp.clip(1.0 + 0.15 * jax.random.normal(splits[4], (N_SEC, D), jnp.float32), 0.25, 1.75)
    route_weight = gaussian(splits[5], (N_SEC, D), D ** -0.5, 0.125, ((0, 8),))
    w_query = gaussian(splits[6], (N_SEC, D, HEADS * HEAD_DIM), D ** -0.5, 0.125, ((0, 8), (2, 4)))
    w_key = gaussian(splits[7], (N_SEC, D, HEADS * HEAD_DIM), (2.0 / D ** 0.5), 0.26367188, ((0, 8), (2, 4)))
    w_value = gaussian(splits[8], (N_SEC, D, HEADS * HEAD_DIM), D ** -0.5, 0.125, ((0, 8), (2, 4)))
    w_out = gaussian(splits[9], (N_SEC, HEADS * HEAD_DIM, D), (4.0 / (HEADS * HEAD_DIM) ** 0.5), 0.52734375, ((0, 8), (2, 4)))
    cache_keys = draw_cache_keys(jax.random.fold_in(splits[12], 71), 0)
    cache_values = gaussian(splits[11], (N_SEC, CACHE, HEADS * HEAD_DIM), 1.0, 6.0, ((0, 8), (2, 4)))
    return dict(tokens=tokens, fresh_tokens=fresh_tokens, route_rows=route_rows, block_list=block_list, norm_gain=norm_gain, route_weight=route_weight, w_query=w_query, w_key=w_key, w_value=w_value, w_out=w_out, cache_keys=cache_keys, cache_values=cache_values)


def attend_all(queries, key_rows, value_rows, row_index, cache_k, cache_v, picks):
    row_count, head_count, head_width = queries.shape
    group_count = picks.shape[0]
    score_scale = 1.0 / math.sqrt(head_width)
    chosen_keys = cache_k.reshape(-1, BLOCK, head_count, head_width)[picks].reshape(group_count, -1, head_count, head_width)
    chosen_values = cache_v.reshape(-1, BLOCK, head_count, head_width)[picks].reshape(group_count, -1, head_count, head_width)
    query_groups = queries.reshape(group_count, -1, head_count, head_width)
    cache_scores = jnp.einsum('crhd,ckhd->chrk', query_groups.astype(jnp.float32), chosen_keys.astype(jnp.float32)) * score_scale
    local_scores = jnp.einsum('qhd,khd->hqk', queries.astype(jnp.float32), key_rows.astype(jnp.float32)) * score_scale
    visible = row_index[None, :] <= row_index[:, None]
    local_scores = jnp.where(visible[None], local_scores, -jnp.inf)
    cache_max = jnp.transpose(lax.optimization_barrier(jnp.max(cache_scores, axis=-1)), (1, 0, 2)).reshape(head_count, row_count)
    row_max = jnp.maximum(cache_max, lax.optimization_barrier(jnp.max(local_scores, axis=-1)))
    group_max = jnp.transpose(row_max.reshape(head_count, group_count, -1), (1, 0, 2))
    cache_weights = jnp.exp(cache_scores - group_max[..., None])
    local_weights = jnp.exp(local_scores - row_max[..., None])
    cache_sum = jnp.transpose(lax.optimization_barrier(jnp.sum(cache_weights, axis=-1)), (1, 0, 2)).reshape(head_count, row_count)
    denom_sum = cache_sum + lax.optimization_barrier(jnp.sum(local_weights, axis=-1))
    cache_probs = cache_weights.astype(jnp.bfloat16).astype(jnp.float32)
    local_probs = local_weights.astype(jnp.bfloat16).astype(jnp.float32)
    from_cache = jnp.einsum('chrk,ckhd->crhd', cache_probs, chosen_values.astype(jnp.float32)).reshape(row_count, head_count, head_width)
    from_local = jnp.einsum('hqk,khd->qhd', local_probs, value_rows.astype(jnp.float32))
    attended = (from_cache + from_local) / jnp.transpose(denom_sum)[:, :, None]
    return attended.astype(jnp.bfloat16).reshape(row_count, head_count * head_width)

def section(operands):
    rows_in, chosen, picks, gain_row, router, query_w, key_w, value_w, output_w, cache_k, cache_v = operands
    row_index = (chosen + GROUP * jnp.arange(GROUPS, dtype=jnp.int32)[:, None]).reshape(-1).astype(jnp.int32)
    picked = rows_in[row_index].astype(jnp.float32)
    mean_square = lax.optimization_barrier(jnp.mean(picked * picked, axis=-1, keepdims=True))
    normed = (picked * lax.rsqrt(mean_square + 1e-05) * gain_row[None, :]).astype(jnp.bfloat16)
    gate_value = jax.nn.sigmoid(jnp.dot(normed, router, preferred_element_type=jnp.float32))
    queries = jnp.dot(normed, query_w, preferred_element_type=jnp.float32).astype(jnp.bfloat16).reshape(-1, HEADS, HEAD_DIM)
    key_rows = jnp.dot(normed, key_w, preferred_element_type=jnp.float32).astype(jnp.bfloat16).reshape(-1, HEADS, HEAD_DIM)
    value_rows = jnp.dot(normed, value_w, preferred_element_type=jnp.float32).astype(jnp.bfloat16).reshape(-1, HEADS, HEAD_DIM)
    attended = attend_all(queries, key_rows, value_rows, row_index, cache_k, cache_v, picks)
    branch = jnp.dot(attended, output_w, preferred_element_type=jnp.float32)
    updated = (picked + gate_value[:, None] * branch).astype(jnp.bfloat16)
    return rows_in.at[row_index].set(updated)

def reference(tokens, fresh_tokens, route_rows, block_list, norm_gain, route_weight, w_query, w_key, w_value, w_out, cache_keys, cache_values):
    stacked = tokens.reshape(N_SEC, TOK_DEV, D)
    results = lax.map(section, (stacked, route_rows, block_list, norm_gain, route_weight, w_query, w_key, w_value, w_out, cache_keys, cache_values))
    shifted = jnp.concatenate([fresh_tokens[None], results[:-1]], axis=0)
    return shifted.reshape(TOKENS, D)
```

```python
import functools
import math

import jax
import jax.numpy as jnp
from jax import lax
from jax.experimental import pallas as pl
from jax.experimental.pallas import tpu as pltpu
from jax.sharding import PartitionSpec as P

HEAD_DIM = 64
BLOCK = 128
LANES = 128
EPS = 1e-05


f32 = jnp.float32
bf16 = jnp.bfloat16
VMEM_SPEC = pl.BlockSpec(memory_space=pltpu.VMEM)
SMEM_SPEC = pl.BlockSpec(memory_space=pltpu.SMEM)
ANY_SPEC = pl.BlockSpec(memory_space=pl.ANY)


def shift_up(shard, axis):
    length = lax.axis_size(axis)
    return lax.ppermute(shard, axis, [(i, i + 1) for i in range(length - 1)])


def ring_step(shard, axis):
    length = lax.axis_size(axis)
    return lax.ppermute(shard, axis, [(i, (i + 1) % length) for i in range(length)])


def dot(a, b):
    return lax.dot_general(a, b, (((1,), (0,)), ((), ())), preferred_element_type=f32)


def dot_nt(a, b):
    return lax.dot_general(a, b, (((1,), (1,)), ((), ())), preferred_element_type=f32)


def dot_tn(a, b):
    return lax.dot_general(a, b, (((0,), (0,)), ((), ())), preferred_element_type=f32)


def hot_rows(route_row, rows):
    picks = route_row.shape[1]
    return lax.broadcasted_iota(jnp.int32, (rows, picks), 0) == route_row


def pick_kernel(groups, group_rows, route_ref, tokens_ref, *outs):
    for slot, group in enumerate(groups):
        hot = hot_rows(route_ref[0, group : group + 1, :], group_rows)
        rows = tokens_ref[slot * group_rows : (slot + 1) * group_rows, :]
        outs[slot][...] = dot_tn(hot.astype(f32).astype(bf16), rows).astype(bf16)


def pick(tokens, route_rows, groups):
    group_count, picks = route_rows.shape[1:]
    group_rows = tokens.shape[0] // group_count
    width = tokens.shape[1]
    span = len(groups)
    assert groups[0] % span == 0 or span == 1
    return pl.pallas_call(
        functools.partial(pick_kernel, groups, group_rows),
        out_shape=[jax.ShapeDtypeStruct((picks, width), bf16)] * span,
        grid=(1,),
        in_specs=[
            pl.BlockSpec(route_rows.shape, lambda i: (0, 0, 0)),
            pl.BlockSpec((span * group_rows, width), lambda i: (groups[0] // span, 0)),
        ],
        out_specs=[pl.BlockSpec((picks, width), lambda i: (0, 0))] * span,
        name="pick",
    )(route_rows, tokens)


def group_kernel(group, shards, sizes, *refs):
    picks, width, key_count, chunk = sizes
    it = iter(refs)
    me_ref, blocks_ref = next(it), next(it)
    x_refs = [next(it) for _ in range(shards)]
    gain_ref, router_ref, route_ref = next(it), next(it), next(it)
    w_refs = [next(it) for _ in range(3)]
    ck_ref, cv_ref = next(it), next(it)
    old_k = [next(it) for _ in range(group)]
    old_v = [next(it) for _ in range(group)]
    att_ref, gate_ref, k_ref, v_ref = next(it), next(it), next(it), next(it)
    wbuf, kbuf, vbuf, qbuf, sbuf = (next(it) for _ in range(5))
    wsem, ksem, vsem = next(it), next(it), next(it)

    w_copies = [pltpu.make_async_copy(w_refs[i], wbuf.at[i], wsem.at[i]) for i in range(3)]
    for copy in w_copies:
        copy.start()
    k_copies, v_copies = [], []
    for j in range(key_count // BLOCK):
        block = pl.multiple_of(blocks_ref[0, group, j] * BLOCK, BLOCK)
        here = pl.ds(j * BLOCK, BLOCK)
        k_copies.append(pltpu.make_async_copy(ck_ref.at[pl.ds(block, BLOCK), :], kbuf.at[here, :], ksem.at[j]))
        v_copies.append(pltpu.make_async_copy(cv_ref.at[pl.ds(block, BLOCK), :], vbuf.at[here, :], vsem.at[j]))
    for copy in k_copies:
        copy.start()
    for copy in v_copies:
        copy.start()

    me = me_ref[0]
    xs = [ref[...].astype(f32) for ref in x_refs]
    square = sum(jnp.sum(x * x, axis=1, keepdims=True) for x in xs)
    inverse = lax.rsqrt(square / (width * shards) + EPS)
    normed, owners, gate = [], [], 0.0
    for s, x in enumerate(xs):
        owner = lax.rem(me - s + shards, shards)
        owners.append(owner)
        piece = (x * inverse * gain_ref[pl.ds(owner, 1), :]).astype(bf16)
        gate = gate + jnp.sum(
            piece.astype(f32) * router_ref[pl.ds(owner, 1), :], axis=1, keepdims=True
        )
        normed.append(piece)
    gate_ref[...] = jnp.broadcast_to(jax.nn.sigmoid(gate), gate_ref.shape)

    def project(i):
        w_copies[i].wait()
        total = 0.0
        for piece, owner in zip(normed, owners):
            rows = pl.ds(pl.multiple_of(owner * width, width), width)
            total = total + dot(piece, wbuf[i, rows, :])
        return total

    qbuf[...] = (project(0).astype(bf16).astype(f32) * (1.0 / math.sqrt(HEAD_DIM))).astype(bf16)
    k_ref[...] = project(1).astype(bf16)
    v_ref[...] = project(2).astype(bf16)

    row = route_ref[0, group : group + 1, :]
    wide = jnp.broadcast_to(row, (picks, picks))
    visible = wide <= jnp.transpose(wide)
    visible2 = jnp.concatenate([visible] * 2, axis=0)
    low = lax.broadcasted_iota(jnp.int32, (picks, LANES), 1) < HEAD_DIM

    for copy in k_copies:
        copy.wait()
    for copy in v_copies:
        copy.wait()

    local_k = list(old_k) + [k_ref]
    local_v = list(old_v) + [v_ref]
    for pair in range(width // LANES):
        lanes = slice(pair * LANES, (pair + 1) * LANES)
        q = qbuf[:, lanes]
        zero = jnp.zeros_like(q)
        q2 = jnp.concatenate([jnp.where(low, q, zero), jnp.where(low, zero, q)], axis=0)
        spans = []
        top = None
        for start in range(0, key_count, chunk):
            spans.append((kbuf, vbuf, start, chunk, start))
        for g in range(group + 1):
            spans.append((local_k[g], local_v[g], 0, picks, key_count + g * picks))
        for n, (kr, _, start, size, at) in enumerate(spans):
            s = dot_nt(q2, kr[start : start + size, lanes])
            if n == len(spans) - 1:
                s = jnp.where(visible2, s, -jnp.inf)
            sbuf[:, at : at + size] = s
            for l in range(0, size, LANES):
                part = s[:, l : l + LANES]
                top = part if top is None else jnp.maximum(top, part)
        peak = jnp.max(top, axis=1, keepdims=True)
        mass, total = 0.0, 0.0
        for _, vr, start, size, at in spans:
            p = jnp.exp(sbuf[:, at : at + size] - peak)
            for l in range(0, size, LANES):
                mass = mass + p[:, l : l + LANES]
            total = total + dot(p.astype(bf16), vr[start : start + size, lanes])
        denom = jnp.sum(mass, axis=1, keepdims=True)
        done = total / denom
        att_ref[:, lanes] = jnp.where(low, done[:picks], done[picks:]).astype(bf16)


def group_step(group, me, block_list, shards, gain, router, route_rows, w3, ck, cv, old_k, old_v):
    picks, width = shards[0].shape
    key_count = block_list.shape[2] * BLOCK
    n = len(shards)
    chunk = min(512, key_count)
    dims = (picks, width, key_count, chunk)
    row_shape = jax.ShapeDtypeStruct((picks, width), bf16)
    total_keys = key_count + (group + 1) * picks
    heads = width // HEAD_DIM
    return pl.pallas_call(
        functools.partial(group_kernel, group, n, dims),
        out_shape=[row_shape, jax.ShapeDtypeStruct((picks, LANES), f32), row_shape, row_shape],
        in_specs=[SMEM_SPEC] * 2
        + [VMEM_SPEC] * (n + 3)
        + [ANY_SPEC] * 5
        + [VMEM_SPEC] * (2 * group),
        out_specs=[VMEM_SPEC] * 4,
        scratch_shapes=[
            pltpu.VMEM((3,) + w3[0].shape, bf16),
            pltpu.VMEM((key_count, width), bf16),
            pltpu.VMEM((key_count, width), bf16),
            pltpu.VMEM((picks, width), bf16),
            pltpu.VMEM((2 * picks, total_keys), f32),
            pltpu.SemaphoreType.DMA((3,)),
            pltpu.SemaphoreType.DMA((key_count // BLOCK,)),
            pltpu.SemaphoreType.DMA((key_count // BLOCK,)),
        ],
        compiler_params=pltpu.CompilerParams(vmem_limit_bytes=32 << 20),
        cost_estimate=pl.CostEstimate(
            flops=2 * picks * width * (3 * width * n + 2 * total_keys) * 4,
            bytes_accessed=2 * (3 * width * width * n + 2 * key_count * width),
            transcendentals=picks * total_keys * heads,
        ),
        name=f"group{group}",
    )(me, block_list, *shards, gain, router, route_rows, *w3, ck, cv, *old_k, *old_v)


def finish_kernel(group, shards, group_rows, me_ref, route_ref, gate_ref, *refs):
    x_refs = refs[:shards]
    w_ref, base_ref, out_ref, wbuf, rbuf, obuf, wsem, rsem, osem = refs[shards:]
    rows = pl.ds(group * group_rows, group_rows)
    w_copy = pltpu.make_async_copy(w_ref, wbuf, wsem)
    r_copy = pltpu.make_async_copy(base_ref.at[rows, :], rbuf, rsem)
    r_copy.start()
    w_copy.start()
    hot = hot_rows(route_ref[0, group : group + 1, :], group_rows)
    hot_f = hot.astype(f32)
    hot_b = hot_f.astype(bf16)
    routed = jnp.sum(hot_f, axis=1, keepdims=True) > 0.5
    r_copy.wait()
    base = rbuf[...]
    own = dot_tn(hot_b, base)
    me = me_ref[0]
    width = x_refs[0].shape[1]
    w_copy.wait()
    branch = 0.0
    for s, ref in enumerate(x_refs):
        owner = lax.rem(me - s + shards, shards)
        branch = branch + dot(ref[...], wbuf[pl.ds(pl.multiple_of(owner * width, width), width), :])
    gate = jnp.concatenate([gate_ref[...]] * (width // LANES), axis=1)
    updated = (own + gate * branch).astype(bf16)
    spread = dot(hot_b, updated)
    obuf[...] = jnp.where(routed, spread, base.astype(f32)).astype(bf16)
    o_copy = pltpu.make_async_copy(obuf, out_ref.at[rows, :], osem)
    o_copy.start()
    o_copy.wait()


def finish(group, me, route_rows, gate, shards, w_out, base):
    picks, width = shards[0].shape
    group_rows = base.shape[0] // route_rows.shape[1]
    n = len(shards)
    return pl.pallas_call(
        functools.partial(finish_kernel, group, n, group_rows),
        out_shape=jax.ShapeDtypeStruct(base.shape, base.dtype),
        in_specs=[SMEM_SPEC] + [VMEM_SPEC] * (2 + n) + [ANY_SPEC] * 2,
        out_specs=ANY_SPEC,
        input_output_aliases={3 + n + 1: 0},
        scratch_shapes=[
            pltpu.VMEM(w_out.shape, bf16),
            pltpu.VMEM((group_rows, width), bf16),
            pltpu.VMEM((group_rows, width), bf16),
            pltpu.SemaphoreType.DMA,
            pltpu.SemaphoreType.DMA,
            pltpu.SemaphoreType.DMA,
        ],
        compiler_params=pltpu.CompilerParams(vmem_limit_bytes=16 << 20),
        cost_estimate=pl.CostEstimate(
            flops=2 * picks * width * width * n,
            bytes_accessed=2 * width * width * n,
            transcendentals=0,
        ),
        name=f"finish{group}",
    )(me, route_rows, gate, *shards, w_out, base)


def body(
    tokens,
    fresh_tokens,
    route_rows,
    block_list,
    norm_gain,
    route_weight,
    w_query,
    w_key,
    w_value,
    w_out,
    cache_keys,
    cache_values,
):
    group_count = route_rows.shape[1]
    width = tokens.shape[1]
    n = lax.axis_size("head")
    me = lax.axis_index("head").astype(jnp.int32).reshape(1)
    gain = norm_gain[0].reshape(n, width)
    router = route_weight[0].astype(f32).reshape(n, width)
    w3 = (w_query[0], w_key[0], w_value[0])
    ck, cv = cache_keys[0], cache_values[0]

    picked = [pick(tokens, route_rows, (g,))[0] for g in range(group_count)]

    passed = shift_up(tokens, "sec")
    passed_route = shift_up(route_rows, "sec")
    passed_w = shift_up(w_out[0], "sec")
    first = lax.axis_index("sec") == 0
    base = jnp.where(first, fresh_tokens, passed)
    passed_route = jnp.where(first, -1, passed_route)

    old_k, old_v, sent = [], [], []
    for g in range(group_count):
        shards = [picked[g]]
        for _ in range(n - 1):
            shards.append(ring_step(shards[-1], "head"))
        attended, gate, key_rows, value_rows = group_step(
            g, me, block_list, shards, gain, router, route_rows, w3, ck, cv, old_k, old_v
        )
        old_k.append(key_rows)
        old_v.append(value_rows)
        sent.append((shift_up(attended, "sec"), shift_up(gate, "sec")))
    for g in range(group_count):
        attended, gate = sent[g]
        shards = [attended]
        for _ in range(n - 1):
            shards.append(ring_step(shards[-1], "head"))
        base = finish(g, me, passed_route, gate, shards, passed_w, base)
    return base


def solution(mesh):
    placed = (
        P("sec", "head"),
        P(None, "head"),
        P("sec", None, None),
        P("sec", None, None),
        P("sec", None),
        P("sec", None),
        P("sec", None, "head"),
        P("sec", None, "head"),
        P("sec", None, "head"),
        P("sec", None, "head"),
        P("sec", None, "head"),
        P("sec", None, "head"),
    )
    return jax.shard_map(
        body, mesh=mesh, in_specs=placed, out_specs=P("sec", "head"), check_vma=False
    )
```

```python
import functools
import math

import jax
import jax.numpy as jnp
from jax import lax
from jax.experimental import pallas as pl
from jax.experimental.pallas import tpu as pltpu
from jax.sharding import PartitionSpec as P

HEAD_DIM = 64
BLOCK = 128
LANES = 128
EPS = 1e-05
STAGE_LIMIT = 32 << 20
LIMIT = 12 << 20


f32 = jnp.float32
bf16 = jnp.bfloat16
VMEM_SPEC = pl.BlockSpec(memory_space=pltpu.VMEM)
SMEM_SPEC = pl.BlockSpec(memory_space=pltpu.SMEM)
HBM_SPEC = pl.BlockSpec(memory_space=pltpu.HBM)


def shift_up(shard, axis):
    length = lax.axis_size(axis)
    return lax.ppermute(shard, axis, [(i, i + 1) for i in range(length - 1)])


def ring_step(shard, axis):
    length = lax.axis_size(axis)
    return lax.ppermute(shard, axis, [(i, (i + 1) % length) for i in range(length)])


def in_hbm(array):
    return pltpu.with_memory_space_constraint(array, pltpu.HBM)


def dot(a, b):
    return lax.dot_general(a, b, (((1,), (0,)), ((), ())), preferred_element_type=f32)


def dot_nt(a, b):
    return lax.dot_general(a, b, (((1,), (1,)), ((), ())), preferred_element_type=f32)


def dot_tn(a, b):
    return lax.dot_general(a, b, (((0,), (0,)), ((), ())), preferred_element_type=f32)


def hot_rows(route_row, rows):
    picks = route_row.shape[1]
    return lax.broadcasted_iota(jnp.int32, (rows, picks), 0) == route_row


def pick_kernel(group_rows, route_ref, tokens_ref, *outs):
    for group, out in enumerate(outs):
        hot = hot_rows(route_ref[0, group : group + 1, :], group_rows)
        rows = tokens_ref[group * group_rows : (group + 1) * group_rows, :]
        out[...] = dot_tn(hot.astype(f32).astype(bf16), rows).astype(bf16)


def pick(tokens, route_rows):
    group_count, picks = route_rows.shape[1:]
    width = tokens.shape[1]
    return pl.pallas_call(
        functools.partial(pick_kernel, tokens.shape[0] // group_count),
        out_shape=[jax.ShapeDtypeStruct((picks, width), bf16)] * group_count,
        in_specs=[VMEM_SPEC] * 2,
        out_specs=[VMEM_SPEC] * group_count,
        compiler_params=pltpu.CompilerParams(vmem_limit_bytes=8 << 20),
        name="pick",
    )(route_rows, tokens)


def group_kernel(group, shards, sizes, *refs):
    picks, width, key_count, per = sizes
    it = iter(refs)
    me_ref, blocks_ref = next(it), next(it)
    x_refs = [next(it) for _ in range(shards)]
    gain_ref, router_ref, route_ref = next(it), next(it), next(it)
    w_refs = [next(it) for _ in range(3)]
    ck_ref, cv_ref = next(it), next(it)
    old_k = [next(it) for _ in range(group)]
    old_v = [next(it) for _ in range(group)]
    old_gate = [next(it) for _ in range(min(group, 1))]
    att_ref, gate_ref, k_ref, v_ref = next(it), next(it), next(it), next(it)
    loads = []
    if group == 0:
        held = [next(it) for _ in range(5)]
    qbuf, sbuf = next(it), next(it)
    if group == 0:
        sems = next(it)
        for i, (src, dst) in enumerate(zip(w_refs + [ck_ref, cv_ref], held)):
            loads.append(pltpu.make_async_copy(src, dst, sems.at[i]))
            loads[-1].start()
        w_refs, (ck_ref, cv_ref) = held[:3], held[3:]

    def ready(i):
        if loads:
            loads[i].wait()

    starts = [
        pl.multiple_of(blocks_ref[0, group, j] * BLOCK, BLOCK) for j in range(key_count // BLOCK)
    ]

    me = me_ref[0]
    xs = [ref[...].astype(f32) for ref in x_refs]
    square = sum(jnp.sum(x * x, axis=1, keepdims=True) for x in xs)
    inverse = lax.rsqrt(square / (width * shards) + EPS)
    normed, owners, gate = [], [], 0.0
    for s, x in enumerate(xs):
        owner = lax.rem(me - s + shards, shards)
        owners.append(owner)
        span = pl.ds(pl.multiple_of(owner * width, width), width)
        piece = (x * inverse * gain_ref[:, span]).astype(bf16)
        gate = gate + jnp.sum(
            piece.astype(f32) * router_ref[:, span].astype(f32), axis=1, keepdims=True
        )
        normed.append(piece)
    gate_row = jnp.transpose(jnp.broadcast_to(jax.nn.sigmoid(gate), (picks, LANES)))[:1, :]
    if old_gate:
        gate_ref[...] = old_gate[0][...]
    else:
        gate_ref[...] = jnp.zeros(gate_ref.shape, f32)
    gate_ref[group : group + 1, :] = gate_row

    def project(i):
        ready(i)
        total = 0.0
        for piece, owner in zip(normed, owners):
            rows = pl.ds(pl.multiple_of(owner * width, width), width)
            total = total + dot(piece, w_refs[i][rows, :])
        return total

    qbuf[...] = (project(0).astype(bf16).astype(f32) * (1.0 / math.sqrt(HEAD_DIM))).astype(bf16)
    k_ref[...] = project(1).astype(bf16)
    v_ref[...] = project(2).astype(bf16)

    row = route_ref[0, group : group + 1, :]
    wide = jnp.broadcast_to(row, (picks, picks))
    visible = wide <= jnp.transpose(wide)
    visible2 = jnp.concatenate([visible] * 2, axis=0)
    low = lax.broadcasted_iota(jnp.int32, (picks, LANES), 1) < HEAD_DIM

    def fetch(ref, span, lanes):
        return jnp.concatenate([ref[pl.ds(at, BLOCK), lanes] for at in span], axis=0)

    ready(3)
    local_k = list(old_k) + [k_ref]
    local_v = list(old_v) + [v_ref]
    for pair in range(width // LANES):
        lanes = slice(pair * LANES, (pair + 1) * LANES)
        q = qbuf[:, lanes]
        zero = jnp.zeros_like(q)
        q2 = jnp.concatenate([jnp.where(low, q, zero), jnp.where(low, zero, q)], axis=0)
        spans = []
        top = None
        for first in range(0, len(starts), per):
            span = starts[first : first + per]
            spans.append((ck_ref, cv_ref, span, len(span) * BLOCK, first * BLOCK))
        for g in range(group + 1):
            spans.append((local_k[g], local_v[g], None, picks, key_count + g * picks))
        for n, (kr, _, span, size, at) in enumerate(spans):
            s = dot_nt(q2, fetch(kr, span, lanes) if span else kr[:, lanes])
            if n == len(spans) - 1:
                s = jnp.where(visible2, s, -jnp.inf)
            sbuf[:, at : at + size] = s
            for l in range(0, size, LANES):
                part = s[:, l : l + LANES]
                top = part if top is None else jnp.maximum(top, part)
        peak = jnp.max(top, axis=1, keepdims=True)
        if pair == 0:
            ready(4)
        mass, total = 0.0, 0.0
        for _, vr, span, size, at in spans:
            p = jnp.exp(sbuf[:, at : at + size] - peak)
            for l in range(0, size, LANES):
                mass = mass + p[:, l : l + LANES]
            total = total + dot(p.astype(bf16), fetch(vr, span, lanes) if span else vr[:, lanes])
        denom = jnp.sum(mass, axis=1, keepdims=True)
        done = total / denom
        att_ref[:, lanes] = jnp.where(low, done[:picks], done[picks:]).astype(bf16)


def group_step(group, me, block_list, shards, gain, router, route_rows, w3, ck, cv, old_k, old_v, old_gate):
    picks, width = shards[0].shape
    key_count = block_list.shape[2] * BLOCK
    n = len(shards)
    dims = (picks, width, key_count, 4)
    row_shape = jax.ShapeDtypeStruct((picks, width), bf16)
    total_keys = key_count + (group + 1) * picks
    heads = width // HEAD_DIM
    big = [jax.ShapeDtypeStruct(a.shape, a.dtype) for a in (*w3, ck, cv)] if group == 0 else []
    return pl.pallas_call(
        functools.partial(group_kernel, group, n, dims),
        out_shape=[row_shape, jax.ShapeDtypeStruct(route_rows.shape[1:], f32), row_shape, row_shape] + big,
        in_specs=[SMEM_SPEC] * 2
        + [VMEM_SPEC] * (n + 3)
        + [HBM_SPEC if group == 0 else VMEM_SPEC] * 5
        + [VMEM_SPEC] * (2 * group + len(old_gate)),
        out_specs=[VMEM_SPEC] * (4 + len(big)),
        scratch_shapes=[
            pltpu.VMEM((picks, width), bf16),
            pltpu.VMEM((2 * picks, total_keys), f32),
        ]
        + [pltpu.SemaphoreType.DMA((5,))] * min(len(big), 1),
        compiler_params=pltpu.CompilerParams(vmem_limit_bytes=STAGE_LIMIT if group == 0 else LIMIT),
        cost_estimate=pl.CostEstimate(
            flops=2 * picks * width * (3 * width * n + 2 * total_keys) * 4,
            bytes_accessed=2 * (3 * width * width * n + 2 * key_count * width),
            transcendentals=picks * total_keys * heads,
        ),
        name=f"group{group}",
    )(me, block_list, *shards, gain, router, route_rows, *w3, ck, cv, *old_k, *old_v, *old_gate)


def finish_kernel(group, shards, group_rows, at_ref, route_ref, gate_ref, *refs):
    x_refs = refs[:shards]
    w_ref, fresh_ref, passed_ref = refs[shards : shards + 3]
    out_ref, rbuf, obuf, rsem, osem = refs[-5:]
    rows = pl.ds(group * group_rows, group_rows)
    me = at_ref[0]
    first = at_ref[1] == 0

    @pl.when(first)
    def _():
        pltpu.make_async_copy(fresh_ref.at[rows, :], rbuf, rsem).start()

    @pl.when(jnp.logical_not(first))
    def _():
        pltpu.make_async_copy(passed_ref.at[rows, :], rbuf, rsem).start()

    width = x_refs[0].shape[1]
    branch = 0.0
    for s, ref in enumerate(x_refs):
        owner = lax.rem(me - s + shards, shards)
        branch = branch + dot(ref[...], w_ref[pl.ds(pl.multiple_of(owner * width, width), width), :])
    route = jnp.where(first, -1, route_ref[0, group : group + 1, :])
    hot_f = hot_rows(route, group_rows).astype(f32)
    hot_b = hot_f.astype(bf16)
    routed = jnp.sum(hot_f, axis=1, keepdims=True) > 0.5
    picks = route.shape[1]
    gate = jnp.transpose(jnp.broadcast_to(gate_ref[group : group + 1, :], (LANES, picks)))
    gate = jnp.concatenate([gate] * (width // LANES), axis=1)
    pltpu.make_async_copy(passed_ref.at[rows, :], rbuf, rsem).wait()
    base = rbuf[...]
    own = dot_tn(hot_b, base)
    updated = (own + gate * branch).astype(bf16)
    spread = dot(hot_b, updated)
    obuf[...] = jnp.where(routed, spread, base.astype(f32)).astype(bf16)
    o_copy = pltpu.make_async_copy(obuf, out_ref.at[rows, :], osem)
    o_copy.start()
    o_copy.wait()


def finish(group, at, route_rows, gates, shards, w_out, fresh, passed, result):
    picks, width = shards[0].shape
    group_rows = passed.shape[0] // route_rows.shape[1]
    n = len(shards)
    more = [] if result is None else [result]
    return pl.pallas_call(
        functools.partial(finish_kernel, group, n, group_rows),
        out_shape=jax.ShapeDtypeStruct(passed.shape, passed.dtype),
        in_specs=[SMEM_SPEC] + [VMEM_SPEC] * (3 + n) + [HBM_SPEC] * (2 + len(more)),
        out_specs=HBM_SPEC,
        input_output_aliases={6 + n: 0} if more else {},
        scratch_shapes=[
            pltpu.VMEM((group_rows, width), bf16),
            pltpu.VMEM((group_rows, width), bf16),
            pltpu.SemaphoreType.DMA,
            pltpu.SemaphoreType.DMA,
        ],
        compiler_params=pltpu.CompilerParams(vmem_limit_bytes=8 << 20),
        cost_estimate=pl.CostEstimate(
            flops=2 * picks * width * width * n,
            bytes_accessed=2 * width * width * n,
            transcendentals=0,
        ),
        name=f"finish{group}",
    )(at, route_rows, gates, *shards, w_out, fresh, passed, *more)


def body(
    tokens,
    fresh_tokens,
    route_rows,
    block_list,
    norm_gain,
    route_weight,
    w_query,
    w_key,
    w_value,
    w_out,
    cache_keys,
    cache_values,
):
    group_count = route_rows.shape[1]
    width = tokens.shape[1]
    n = lax.axis_size("head")
    at = jnp.stack([lax.axis_index("head"), lax.axis_index("sec")]).astype(jnp.int32)
    gain, router = norm_gain, route_weight
    w3 = tuple(in_hbm(w[0]) for w in (w_query, w_key, w_value))
    ck, cv = in_hbm(cache_keys[0]), in_hbm(cache_values[0])

    picked = pick(tokens, route_rows)
    passed = shift_up(tokens, "sec")
    passed_route = shift_up(route_rows, "sec")
    passed_w = shift_up(w_out[0], "sec")

    old_k, old_v, gates, sent = [], [], [], []
    for g in range(group_count):
        shards = [picked[g]]
        for _ in range(n - 1):
            shards.append(ring_step(shards[-1], "head"))
        attended, gate, key_rows, value_rows, *held = group_step(
            g, at, block_list, shards, gain, router, route_rows, w3, ck, cv, old_k, old_v, gates
        )
        old_k.append(key_rows)
        old_v.append(value_rows)
        gates = [gate]
        if held:
            w3, ck, cv = held[:3], held[3], held[4]
        sent.append(shift_up(attended, "sec"))
    passed_gates = shift_up(gates[0], "sec")
    result = None
    for g in range(group_count):
        shards = [sent[g]]
        for _ in range(n - 1):
            shards.append(ring_step(shards[-1], "head"))
        result = finish(
            g, at, passed_route, passed_gates, shards, passed_w, fresh_tokens, passed, result
        )
    return result


def solution(mesh):
    placed = (
        P("sec", "head"),
        P(None, "head"),
        P("sec", None, None),
        P("sec", None, None),
        P("sec", None),
        P("sec", None),
        P("sec", None, "head"),
        P("sec", None, "head"),
        P("sec", None, "head"),
        P("sec", None, "head"),
        P("sec", None, "head"),
        P("sec", None, "head"),
    )
    return jax.shard_map(
        body, mesh=mesh, in_specs=placed, out_specs=P("sec", "head"), check_vma=False
    )
```
